32 devices in a mesh: dp: 4 (over z), ulysses: 8 (over y, x, core).
Axes of the slice: x: 2, y: 2, z: 4, core: 2. Of those that a mesh axis runs over, the one named last changes fastest.
Arguments:
- q_raw: bfloat16 [4, 1024, 3072], P('dp', 'ulysses')
- k_raw: bfloat16 [4, 1024, 3072], P('dp', 'ulysses')
- values: bfloat16 [4, 1024, 3072], P('dp', 'ulysses'), may hold values from -6 to 6
- grad_out: bfloat16 [4, 1024, 3072], P('dp', 'ulysses'), may hold values from -6 to 6
- q_gain: float32 [128], replicated
- k_gain: float32 [128], replicated
- block_masks: int32 [24, 8, 8], replicated, may hold values from 0 to 1, as said below
Outputs:
- grad_q_raw: bfloat16 [4, 1024, 3072], P('dp', 'ulysses')
- grad_k_raw: bfloat16 [4, 1024, 3072], P('dp', 'ulysses')
- grad_values: bfloat16 [4, 1024, 3072], P('dp', 'ulysses')
- gain_grads: float32 [2, 128], replicated
The draws below stay inside these ranges and needn't reach their ends.
Inputs may be any that keep to these rules, and one draw needn't show every extreme that they name: `block_masks`: every diagonal block is 1. A third of the heads are dense with some blocks missing, a third keep a band of neighbouring blocks, a third keep blocks a fixed stride apart; which heads are which is drawn.
All inputs are finite; a program needn't handle non-finite values.
Results may differ from the reference program's by a relative error of at most 0.0045.
The reference program's roundings to bfloat16 on the way count: a program that leaves them out, or rounds other values in their place, can miss the bound.
Values may be sent and summed in bfloat16 or wider, within the bound.
A program may use at most 64 MiB of HBM per device.

```python
import jax
import jax.numpy as jnp
from jax import lax

HEADS = 24
HEAD_DIM = 128
BLOCK = 128
SEQ = 1024
VIDEOS = 4
NB = 8


def keys_float(key):
    return jax.random.normal(jax.random.fold_in(key, 31), (VIDEOS, SEQ, HEADS * HEAD_DIM), jnp.float32)


def draw_k_raw(key, part):
    return keys_float(key).astype(jnp.bfloat16)


def draw_q_raw(key, part):
    fresh = jax.random.normal(jax.random.fold_in(key, 32), (VIDEOS, SEQ, HEADS * HEAD_DIM), jnp.float32)
    return fresh.astype(jnp.bfloat16)


def draw_q_gain(key, part):
    return jax.random.uniform(jax.random.fold_in(key, 33), (HEAD_DIM,), jnp.float32, 0.5, 1.6)


def draw_k_gain(key, part):
    return jax.random.uniform(jax.random.fold_in(key, 34), (HEAD_DIM,), jnp.float32, 0.5, 1.6)


def draw_block_masks(key, part):
    base = jax.random.fold_in(key, 41)
    kinds = jax.random.permutation(jax.random.fold_in(base, 1), HEADS) % 3
    rows = jnp.arange(NB)[:, None]
    cols = jnp.arange(NB)[None, :]
    band = max(1, NB // 16)
    period = max(2, NB // 4)
    near = jnp.abs(rows - cols) <= band
    frames = (rows - cols) % period == 0
    roll = jax.random.randint(jax.random.fold_in(base, 2), (HEADS, NB, NB), 0, 10)
    kind_cube = kinds[:, None, None]
    chosen = jnp.where(kind_cube == 0, roll >= 2, jnp.where(kind_cube == 1, near[None] & (roll >= 1), frames[None] & (roll >= 1)))
    return (chosen | (rows == cols)[None]).astype(jnp.int32)


def steps_of(key, dims, shards, least, top_value):
    loudness, own = 1.0, jax.random.fold_in(key, 6)
    for axis_at, blocks in shards:
        heights = jnp.exp(jax.random.uniform(jax.random.fold_in(own, axis_at), (blocks,), jnp.float32, least / len(shards), top_value / len(shards)))
        loudness = loudness * jnp.repeat(heights, dims[axis_at] // blocks).reshape([-1 if axis == axis_at else 1 for axis in range(len(dims))])
    return loudness


def normal_values(stream_key, shape, width, reach, shards=(), dtype=jnp.bfloat16):
    values = jax.random.normal(stream_key, shape, jnp.float32) * width
    if len(shards) > 0:
        values = steps_of(stream_key, shape, shards, -0.22, 0.18) * values
    return jnp.clip(values, min=-reach, max=reach).astype(dtype)


def setup_inputs(seed: int = 0) -> dict:
    key_of = jax.random.split(jax.random.key(seed), 8)
    return {
        "q_raw": draw_q_raw(jax.random.fold_in(key_of[7], 71), 0),
        "k_raw": draw_k_raw(jax.random.fold_in(key_of[7], 71), 0),
        "values": normal_values(key_of[2], (VIDEOS, SEQ, HEADS * HEAD_DIM), 1.0, 6.0, ((0, 4), (1, 8))),
        "grad_out": normal_values(key_of[3], (VIDEOS, SEQ, HEADS * HEAD_DIM), 1.0, 6.0, ((0, 4), (1, 8))),
        "q_gain": draw_q_gain(jax.random.fold_in(key_of[7], 71), 0),
        "k_gain": draw_k_gain(jax.random.fold_in(key_of[7], 71), 0),
        "block_masks": draw_block_masks(jax.random.fold_in(key_of[7], 71), 0),
    }


norm_eps = 1e-06
neg_fill = -1e+30

def rms_norm(raw, gain):
    raw_float = raw.astype(jnp.float32)
    spread = jnp.sqrt(lax.optimization_barrier(jnp.mean(raw_float * raw_float, axis=-1, keepdims=True)) + norm_eps)
    return (raw_float, spread, (raw_float / spread * gain).astype(jnp.bfloat16))

def norm_back(raw_float, spread, gain, grad_normed):
    inner = lax.optimization_barrier(jnp.sum(gain * grad_normed * raw_float, axis=-1, keepdims=True))
    return gain * grad_normed / spread - raw_float * inner / (HEAD_DIM * spread ** 3)

def one_head(operands, q_gain, k_gain):
    q_head, k_head, v_head, out_head, mask_head = operands
    q_float, q_spread, q_normed = rms_norm(q_head, q_gain)
    k_float, k_spread, k_normed = rms_norm(k_head, k_gain)
    allowed = jnp.repeat(jnp.repeat(mask_head, BLOCK, 0), BLOCK, 1) > 0
    score_scale = HEAD_DIM ** (-0.5)
    scores = jnp.dot(q_normed, k_normed.T, preferred_element_type=jnp.float32) * score_scale
    scores = jnp.where(allowed, scores, neg_fill)
    peak = lax.optimization_barrier(jnp.max(scores, axis=1, keepdims=True))
    weights = jnp.where(allowed, jnp.exp(scores - peak), 0.0)
    weights = weights / lax.optimization_barrier(jnp.sum(weights, axis=1, keepdims=True))
    grad_weights = jnp.dot(out_head, v_head.T, preferred_element_type=jnp.float32)
    row_delta = lax.optimization_barrier(jnp.sum(weights * grad_weights, axis=1, keepdims=True))
    grad_scores = weights * (grad_weights - row_delta)
    weights_half = weights.astype(jnp.bfloat16)
    scores_half = grad_scores.astype(jnp.bfloat16)
    grad_v = jnp.dot(weights_half.T, out_head, preferred_element_type=jnp.float32)
    grad_qn = jnp.dot(scores_half, k_normed, preferred_element_type=jnp.float32) * score_scale
    grad_kn = jnp.dot(scores_half.T, q_normed, preferred_element_type=jnp.float32) * score_scale
    grad_q = norm_back(q_float, q_spread, q_gain, grad_qn)
    grad_k = norm_back(k_float, k_spread, k_gain, grad_kn)
    gain_q = lax.optimization_barrier(jnp.sum(grad_qn * q_float / q_spread, axis=0))
    gain_k = lax.optimization_barrier(jnp.sum(grad_kn * k_float / k_spread, axis=0))
    return (grad_q, grad_k, grad_v, jnp.stack([gain_q, gain_k]))

def split_heads(array):
    return array.reshape(SEQ, HEADS, HEAD_DIM).transpose(1, 0, 2)

def join_heads(array):
    return array.transpose(1, 0, 2).reshape(SEQ, HEADS * HEAD_DIM).astype(jnp.bfloat16)

def reference(q_raw, k_raw, values, grad_out, q_gain, k_gain, block_masks):
    grads_q = []
    grads_k = []
    grads_v = []
    gain_total = jnp.zeros((2, HEAD_DIM), jnp.float32)
    for video_index in range(VIDEOS):
        operands = (split_heads(q_raw[video_index]), split_heads(k_raw[video_index]), split_heads(values[video_index]), split_heads(grad_out[video_index]), block_masks)
        grad_q, grad_k, grad_v, gain_parts = lax.map(lambda ops: one_head(ops, q_gain, k_gain), operands)
        grads_q.append(join_heads(grad_q))
        grads_k.append(join_heads(grad_k))
        grads_v.append(join_heads(grad_v))
        gain_total = gain_total + lax.optimization_barrier(jnp.sum(gain_parts, axis=0))
    gain_grads = gain_total * (VIDEOS * SEQ * HEADS) ** (-0.5)
    return (jnp.stack(grads_q), jnp.stack(grads_k), jnp.stack(grads_v), gain_grads)
```

```python
import functools
import math

import jax
import jax.numpy as jnp
from jax import lax
from jax.experimental import pallas as pl
from jax.experimental.pallas import tpu as pltpu
from jax.sharding import PartitionSpec as P

HEADS = 24
HEAD_DIM = 128
SPLITS = 8
BLOCK = 128
TILE = 512
ITEMS = 32


norm_eps = 1e-06
neg_fill = -1e30


def rms_norm(raw, gain):
    raw_float = raw.astype(jnp.float32)
    spread = jnp.sqrt(jnp.mean(raw_float * raw_float, axis=-1, keepdims=True) + norm_eps)
    return (raw_float, spread, (raw_float / spread * gain).astype(jnp.bfloat16))


def norm_back(raw_float, spread, gain, grad_normed):
    inner = jnp.sum(gain * grad_normed * raw_float, axis=-1, keepdims=True)
    return gain * grad_normed / spread - raw_float * inner / (HEAD_DIM * spread**3)


def dot_rows(left_side, right_side):
    return lax.dot_general(
        left_side, right_side, (((1,), (1,)), ((), ())), preferred_element_type=jnp.float32
    )


def dot_cols(left_side, right_side):
    return lax.dot_general(
        left_side, right_side, (((0,), (0,)), ((), ())), preferred_element_type=jnp.float32
    )


def rows_of(source, tile_index):
    return lax.dynamic_slice_in_dim(source, tile_index * TILE, TILE, 0)


def add_rows(target, addend, tile_index):
    return lax.dynamic_update_slice_in_dim(
        target, rows_of(target, tile_index) + addend, tile_index * TILE, 0
    )


def plan_items(block_masks, unit_count):
    block_count = block_masks.shape[1]
    per_unit = ITEMS // unit_count
    head_ids = jnp.arange(HEADS, dtype=jnp.int32)
    weight = jnp.sum(block_masks, axis=(1, 2))
    order = jnp.argsort(-(weight * HEADS + head_ids))
    heavy_heads = order[:SPLITS]
    light_heads = order[SPLITS:]
    counter = jnp.arange(2 * SPLITS, dtype=jnp.int32)
    item_head = jnp.concatenate([heavy_heads[counter // 2], light_heads])
    item_half = jnp.concatenate([1 + counter % 2, jnp.zeros((HEADS - SPLITS,), jnp.int32)])
    upper = jnp.sum(block_masks[:, : block_count // 2, :], axis=(1, 2))
    lower = weight - upper
    item_weight = jnp.where(
        item_half == 0,
        weight[item_head],
        jnp.where(item_half == 1, upper[item_head], lower[item_head]),
    )
    ranked = jnp.argsort(-(item_weight * ITEMS + jnp.arange(ITEMS, dtype=jnp.int32)))
    places = jnp.arange(ITEMS, dtype=jnp.int32)
    rounds = places // unit_count
    column = places % unit_count
    device = jnp.where(rounds % 2 == 0, column, unit_count - 1 - column)
    target = device * per_unit + rounds
    plan_head = jnp.zeros((ITEMS,), jnp.int32).at[target].set(item_head[ranked])
    plan_half = jnp.zeros((ITEMS,), jnp.int32).at[target].set(item_half[ranked])
    return (plan_head, plan_half)


def item_grads(columns, mask_head, half_code, q_gain, k_gain):
    seq_len = columns.shape[0]
    q_float, q_spread, q_normed = rms_norm(columns[:, :HEAD_DIM], q_gain)
    k_float, k_spread, k_normed = rms_norm(columns[:, HEAD_DIM : 2 * HEAD_DIM], k_gain)
    v_rows = columns[:, 2 * HEAD_DIM : 3 * HEAD_DIM]
    o_grads = columns[:, 3 * HEAD_DIM :]
    tile_count = seq_len // TILE
    tile_blocks = TILE // BLOCK
    active = (
        jnp.max(mask_head.reshape(tile_count, tile_blocks, tile_count, tile_blocks), axis=(1, 3))
        > 0
    )
    first_tile = jnp.where(half_code == 2, tile_count // 2, 0)
    last_tile = jnp.where(half_code == 1, tile_count // 2, tile_count)
    score_scale = HEAD_DIM ** (-0.5)

    def allowed_at(row_tile, col_tile):
        blocks = lax.dynamic_slice(
            mask_head, (row_tile * tile_blocks, col_tile * tile_blocks), (tile_blocks, tile_blocks)
        )
        return jnp.repeat(jnp.repeat(blocks, BLOCK, 0), BLOCK, 1) > 0

    def query_tile(row_tile, carry):
        grad_qn, grad_kn, grad_v = carry
        q_tile = rows_of(q_normed, row_tile)
        o_tile = rows_of(o_grads, row_tile)

        def stats_step(col_tile, stats):

            def stats_visit(stats_in):
                run_max, run_sum, run_dot = stats_in
                allowed = allowed_at(row_tile, col_tile)
                scores = jnp.where(
                    allowed, dot_rows(q_tile, rows_of(k_normed, col_tile)) * score_scale, neg_fill
                )
                grad_weights = dot_rows(o_tile, rows_of(v_rows, col_tile))
                new_max = jnp.maximum(run_max, jnp.max(scores, axis=1, keepdims=True))
                weights = jnp.where(allowed, jnp.exp(scores - new_max), 0.0)
                rescale = jnp.exp(run_max - new_max)
                return (
                    new_max,
                    run_sum * rescale + jnp.sum(weights, axis=1, keepdims=True),
                    run_dot * rescale + jnp.sum(weights * grad_weights, axis=1, keepdims=True),
                )

            return lax.cond(
                active[row_tile, col_tile], stats_visit, lambda unchanged: unchanged, stats
            )

        start = (
            jnp.full((TILE, 1), neg_fill, jnp.float32),
            jnp.zeros((TILE, 1), jnp.float32),
            jnp.zeros((TILE, 1), jnp.float32),
        )
        run_max, run_sum, run_dot = lax.fori_loop(0, tile_count, stats_step, start)
        log_total = run_max + jnp.log(run_sum)
        row_delta = run_dot / run_sum

        def grad_step(col_tile, inner):

            def grad_visit(inner_in):
                tile_dq, grad_keys, grad_vals = inner_in
                allowed = allowed_at(row_tile, col_tile)
                k_tile = rows_of(k_normed, col_tile)
                v_tile = rows_of(v_rows, col_tile)
                scores = jnp.where(allowed, dot_rows(q_tile, k_tile) * score_scale, neg_fill)
                weights = jnp.where(allowed, jnp.exp(scores - log_total), 0.0)
                grad_weights = dot_rows(o_tile, v_tile)
                grad_scores = weights * (grad_weights - row_delta)
                weights_half = weights.astype(jnp.bfloat16)
                scores_half = grad_scores.astype(jnp.bfloat16)
                tile_dq = (
                    tile_dq
                    + jnp.dot(scores_half, k_tile, preferred_element_type=jnp.float32) * score_scale
                )
                grad_keys = add_rows(
                    grad_keys, dot_cols(scores_half, q_tile) * score_scale, col_tile
                )
                grad_vals = add_rows(grad_vals, dot_cols(weights_half, o_tile), col_tile)
                return (tile_dq, grad_keys, grad_vals)

            return lax.cond(
                active[row_tile, col_tile], grad_visit, lambda unchanged: unchanged, inner
            )

        tile_dq, grad_kn, grad_v = lax.fori_loop(
            0, tile_count, grad_step, (jnp.zeros((TILE, HEAD_DIM), jnp.float32), grad_kn, grad_v)
        )
        grad_qn = lax.dynamic_update_slice_in_dim(grad_qn, tile_dq, row_tile * TILE, 0)
        return (grad_qn, grad_kn, grad_v)

    empty = jnp.zeros((seq_len, HEAD_DIM), jnp.float32)
    grad_qn, grad_kn, grad_v = lax.fori_loop(
        first_tile, last_tile, query_tile, (empty, empty, empty)
    )
    grad_q = norm_back(q_float, q_spread, q_gain, grad_qn)
    grad_k = norm_back(k_float, k_spread, k_gain, grad_kn)
    gain_part = jnp.stack(
        [
            jnp.sum(grad_qn * q_float / q_spread, axis=0),
            jnp.sum(grad_kn * k_float / k_spread, axis=0),
        ]
    )
    return (jnp.concatenate([grad_q, grad_k, grad_v], axis=1), gain_part)


def body(q_raw, k_raw, values, grad_out, q_gain, k_gain, block_masks):
    unit_count = lax.axis_size("ulysses")
    group_count = lax.axis_size("dp")
    device_rank = lax.axis_index("ulysses")
    videos_here, tok_rows, width = q_raw.shape
    seq_len = tok_rows * unit_count
    per_unit = ITEMS // unit_count
    item_heads, item_halves = plan_items(block_masks, unit_count)
    stacked = jnp.concatenate(
        [
            operand.reshape(videos_here, tok_rows, HEADS, HEAD_DIM)
            for operand in (q_raw, k_raw, values, grad_out)
        ],
        axis=3,
    )
    picked = jnp.take(stacked, item_heads, axis=2)
    outgoing = picked.transpose(2, 0, 1, 3).reshape(
        unit_count, per_unit, videos_here, tok_rows, 4 * HEAD_DIM
    )
    arrived = lax.all_to_all(outgoing, "ulysses", split_axis=0, concat_axis=3, tiled=True)
    results = []
    gain_total = jnp.zeros((2, HEAD_DIM), jnp.float32)
    for item_slot in range(per_unit):
        item_index = device_rank * per_unit + item_slot
        head_index = item_heads[item_index]
        half_code = item_halves[item_index]
        mask_head = lax.dynamic_index_in_dim(block_masks, head_index, 0, keepdims=False)
        item_grad, gain_part = item_grads(
            arrived[0, item_slot, 0], mask_head, half_code, q_gain, k_gain
        )
        video_rows = [item_grad]
        gain_total = gain_total + gain_part
        results.append(jnp.stack(video_rows))
    backward = jnp.stack(results)[None]
    returned = lax.all_to_all(
        backward.astype(jnp.bfloat16), "ulysses", split_axis=3, concat_axis=0, tiled=True
    ).astype(backward.dtype)
    returned = returned.reshape(ITEMS, videos_here, tok_rows, 3 * HEAD_DIM)
    selector = (item_heads[:, None] == jnp.arange(HEADS)[None, :]).astype(jnp.float32)
    merged = jnp.einsum("ih,ivtc->vthc", selector, returned, precision=lax.Precision.HIGHEST)
    grad_q_raw = merged[..., :HEAD_DIM].reshape(videos_here, tok_rows, width).astype(jnp.bfloat16)
    grad_k_raw = (
        merged[..., HEAD_DIM : 2 * HEAD_DIM]
        .reshape(videos_here, tok_rows, width)
        .astype(jnp.bfloat16)
    )
    grad_values = (
        merged[..., 2 * HEAD_DIM :].reshape(videos_here, tok_rows, width).astype(jnp.bfloat16)
    )
    summed = lax.psum(gain_total, ("dp", "ulysses"))
    gain_grads = summed * (group_count * videos_here * seq_len * HEADS) ** (-0.5)
    return (grad_q_raw, grad_k_raw, grad_values, gain_grads)


QUERY_TILE = 256
KERNEL_BYTES = 24 * 2**20
MESH = pl.DeviceIdType.MESH


def aligned(index, size):
    return pl.ds(pl.multiple_of(index * size, size), size)


def head_work(slot, arrived, results, gain_acc, gains, scratch):
    bias, q_norm, k_norm, k_cols, grad_qn, grad_kn, grad_v, scores, grads, probs_half, grads_half = scratch
    _, units, _, tok_rows, _ = arrived.shape
    seq_len = units * tok_rows
    block_count = seq_len // BLOCK
    tile_units = QUERY_TILE // tok_rows
    score_scale = HEAD_DIM ** (-0.5)
    exponent_scale = score_scale * math.log2(math.e)

    def rows_for(which):
        return arrived[slot, :, which].reshape(seq_len, HEAD_DIM)

    def put(which, grad):
        results[slot, :, which] = grad.astype(jnp.bfloat16).reshape(units, tok_rows, HEAD_DIM)

    def normed(which):
        raw = rows_for(which).astype(jnp.float32)
        inverse = 1.0 / jnp.sqrt(jnp.mean(raw * raw, axis=1, keepdims=True) + norm_eps)
        return raw * inverse * gains[which][...]

    q_norm[...] = normed(0).astype(jnp.bfloat16)
    k_float = normed(1)
    k_norm[...] = k_float.astype(jnp.bfloat16)
    k_cols[...] = k_float.T.astype(jnp.bfloat16)
    grad_kn[...] = jnp.zeros_like(grad_kn)
    grad_v[...] = jnp.zeros_like(grad_v)

    def tile_step(tile, carry):
        rows = aligned(tile, QUERY_TILE)
        q_tile = q_norm[rows, :]
        o_tile = arrived[slot, pl.ds(tile * tile_units, tile_units), 3].reshape(QUERY_TILE, HEAD_DIM)
        shifts = bias[:, rows]
        peak = jnp.full((1, QUERY_TILE), -jnp.inf, jnp.float32)
        for block in range(block_count):
            keys = pl.ds(block * BLOCK, BLOCK)
            block_scores = dot_rows(k_norm[keys, :], q_tile)
            scores[keys, :] = block_scores
            block_peak = jnp.max(block_scores, axis=0, keepdims=True) * exponent_scale
            peak = jnp.maximum(peak, block_peak + shifts[block : block + 1, :])
        total = jnp.zeros((1, QUERY_TILE), jnp.float32)
        row_dot = jnp.zeros((1, QUERY_TILE), jnp.float32)
        for block in range(block_count):
            keys = pl.ds(block * BLOCK, BLOCK)
            offset = shifts[block : block + 1, :] - peak
            weights = jnp.exp2(scores[keys, :] * exponent_scale + offset)
            grad_weights = dot_rows(arrived[slot, block, 2], o_tile)
            scores[keys, :] = weights
            grads[keys, :] = grad_weights
            total = total + jnp.sum(weights, axis=0, keepdims=True)
            row_dot = row_dot + jnp.sum(weights * grad_weights, axis=0, keepdims=True)
        inverse = 1.0 / total
        delta = row_dot * inverse
        for block in range(block_count):
            keys = pl.ds(block * BLOCK, BLOCK)
            weights = scores[keys, :] * inverse
            probs_half[keys, :] = weights.astype(jnp.bfloat16)
            grads_half[keys, :] = (weights * (grads[keys, :] - delta)).astype(jnp.bfloat16)
        grad_v[...] += jnp.dot(probs_half[...], o_tile, preferred_element_type=jnp.float32)
        grad_kn[...] += jnp.dot(grads_half[...], q_tile, preferred_element_type=jnp.float32)
        turned = jnp.dot(k_cols[...], grads_half[...], preferred_element_type=jnp.float32)
        grad_qn[rows, :] = turned.T
        return carry

    lax.fori_loop(0, seq_len // QUERY_TILE, tile_step, 0)
    put(2, grad_v[...])
    for which, grad_normed in ((0, grad_qn), (1, grad_kn)):
        raw = rows_for(which).astype(jnp.float32)
        inverse = 1.0 / jnp.sqrt(jnp.mean(raw * raw, axis=1, keepdims=True) + norm_eps)
        unit = raw * inverse
        grad = grad_normed[...] * score_scale
        gain_acc[which : which + 1, :] += jnp.sum(grad * unit, axis=0, keepdims=True)
        scaled = grad * gains[which][...]
        inner = jnp.mean(scaled * unit, axis=1, keepdims=True)
        put(which, (scaled - unit * inner) * inverse)


def exchange_kernel(
    units, groups, gain_scale,
    q_raw, k_raw, values, grad_out, q_gain_in, k_gain_in, masks_in,
    landed, out_gain,
    staged, arrived, results, gain_units, gain_groups, gain_acc,
    stage_sem, in_send, in_recv, in_own, out_send, out_recv, out_own,
    unit_send, unit_recv, group_send, group_recv, small_sem, q_gain, k_gain, masks, *scratch,
):
    me = lax.axis_index("ulysses")
    group = lax.axis_index("dp")
    slots = arrived.shape[0]
    sources = (q_raw, k_raw, values, grad_out)
    bits = units.bit_length() - 1
    group_bits = groups.bit_length() - 1

    def flipped(index, offset, count):
        places = (lax.rem(index // 2**bit + offset // 2**bit, 2) * 2**bit for bit in range(count))
        return sum(places, jnp.int32(0))

    def unit_at(offset):
        return flipped(me, offset, bits)

    offsets = sorted(range(1, units), key=lambda offset: (-(offset // 2).bit_count(), offset % 2, offset))

    def stage(slot, owner, which):
        return pltpu.make_async_copy(
            sources[which].at[0, :, aligned(owner * slots + slot, HEAD_DIM)],
            staged.at[slot, owner, which],
            stage_sem.at[slot],
        )

    def remote(source, target, send_sem, recv_sem, device):
        return pltpu.make_async_remote_copy(
            src_ref=source,
            dst_ref=target,
            send_sem=send_sem,
            recv_sem=recv_sem,
            device_id=device,
            device_id_type=MESH,
        )

    def inward(slot, offset):
        owner = unit_at(offset)
        return remote(
            staged.at[slot, owner], arrived.at[slot, me],
            in_send.at[slot, offset], in_recv.at[slot, offset], {"ulysses": owner},
        )

    def inward_own(slot, which):
        return pltpu.make_async_copy(
            sources[which].at[0, :, aligned(me * slots + slot, HEAD_DIM)],
            arrived.at[slot, me, which],
            in_own.at[slot, which],
        )

    def inward_from(slot, offset):
        owner = unit_at(offset)
        place = arrived.at[slot, owner]
        return remote(place, place, in_send.at[slot, offset], in_recv.at[slot, offset], {"ulysses": owner})

    def outward(slot, offset):
        owner = unit_at(offset)
        return remote(
            results.at[slot, owner], landed.at[me * slots + slot],
            out_send.at[slot, offset], out_recv.at[slot, offset], {"ulysses": owner},
        )

    def outward_own(slot):
        return pltpu.make_async_copy(
            results.at[slot, me], landed.at[me * slots + slot], out_own.at[slot]
        )

    def outward_from(slot, offset):
        owner = unit_at(offset)
        place = landed.at[owner * slots + slot]
        return remote(place, place, out_send.at[slot, offset], out_recv.at[slot, offset], {"ulysses": owner})

    def unit_gain(place, offset):
        block = gain_units.at[place]
        return remote(block, block, unit_send.at[offset], unit_recv.at[offset], {"ulysses": unit_at(offset)})

    def group_gain(bit):
        return remote(
            gain_groups.at[bit, 0], gain_groups.at[bit, 1],
            group_send.at[bit], group_recv.at[bit], {"dp": flipped(group, 2**bit, group_bits)},
        )

    small_copies = [
        pltpu.make_async_copy(source, target, small_sem.at[place])
        for place, (source, target) in enumerate(
            ((q_gain_in, q_gain), (k_gain_in, k_gain), (masks_in, masks))
        )
    ]
    barrier = pltpu.get_barrier_semaphore()
    for offset in offsets:
        pl.semaphore_signal(barrier, inc=1, device_id={"ulysses": unit_at(offset)}, device_id_type=MESH)
    for bit in range(group_bits):
        pl.semaphore_signal(
            barrier, inc=1, device_id={"dp": flipped(group, 2**bit, group_bits)}, device_id_type=MESH
        )

    def fetch_slot(slot, carry):
        for owner in range(units):
            for which in range(4):
                stage(slot, owner, which).start()
        return carry

    lax.fori_loop(0, slots, fetch_slot, 0)
    for copy in small_copies:
        copy.start()
    for slot in range(slots):
        for which in range(4):
            inward_own(slot, which).start()
    gain_acc[...] = jnp.zeros_like(gain_acc)
    pl.semaphore_wait(barrier, units - 1 + group_bits)

    def send_slot(slot, carry):
        pltpu.make_async_copy(staged.at[slot], staged.at[slot], stage_sem.at[slot]).wait()
        for offset in offsets:
            inward(slot, offset).start()
        return carry

    lax.fori_loop(0, slots, send_slot, 0)
    for copy in small_copies:
        copy.wait()
    bias = scratch[0]
    block_count = masks.shape[0]

    def work_slot(slot, carry):
        columns = lax.broadcasted_iota(jnp.int32, (block_count, HEADS), 1)
        for block in range(block_count):
            allowed = jnp.where(columns == me * slots + slot, masks[block].astype(jnp.float32), 0.0)
            allowed = jnp.sum(allowed, axis=1, keepdims=True)
            shift = jnp.where(allowed > 0.0, 0.0, -jnp.inf)
            bias[:, block * BLOCK : (block + 1) * BLOCK] = jnp.broadcast_to(shift, (block_count, BLOCK))
        for which in range(4):
            inward_own(slot, which).wait()
        for offset in offsets:
            inward_from(slot, offset).wait_recv()
        head_work(slot, arrived, results, gain_acc, (q_gain, k_gain), scratch)

        @pl.when(slot == slots - 1)
        def _():
            gain_units[me] = gain_acc[...]
            for offset in offsets:
                unit_gain(me, offset).start()

        for offset in offsets:
            outward(slot, offset).start()
        outward_own(slot).start()
        return carry

    lax.fori_loop(0, slots, work_slot, 0)

    for offset in offsets:
        unit_gain(unit_at(offset), offset).wait_recv()
    gain_sum = jnp.sum(gain_units[...], axis=0)
    for bit in range(group_bits):
        gain_groups[bit, 0] = gain_sum
        group_gain(bit).start()
        group_gain(bit).wait_recv()
        gain_sum = gain_sum + gain_groups[bit, 1]
    out_gain[...] = gain_sum[:2] * gain_scale

    def drain_slot(slot, carry):
        for offset in offsets:
            inward(slot, offset).wait_send()
            outward(slot, offset).wait_send()
            outward_from(slot, offset).wait_recv()
        outward_own(slot).wait()
        return carry

    lax.fori_loop(0, slots, drain_slot, 0)
    for offset in offsets:
        unit_gain(me, offset).wait_send()
    for bit in range(group_bits):
        group_gain(bit).wait_send()


def hand_on_kernel(landed, gain_in, out_q, out_k, out_v, out_gain, sems, gain_sem):
    targets = (out_q, out_k, out_v)
    gain_copy = pltpu.make_async_copy(gain_in, out_gain, gain_sem)
    gain_copy.start()
    for head in range(landed.shape[0]):
        for which in range(3):
            pltpu.make_async_copy(
                landed.at[head, which],
                targets[which].at[0, :, pl.ds(head * HEAD_DIM, HEAD_DIM)],
                sems.at[which],
            ).start()
    for which in range(3):
        pltpu.make_async_copy(targets[which], targets[which], sems.at[which]).wait()
    gain_copy.wait()


def exchange_body(q_raw, k_raw, values, grad_out, q_gain, k_gain, block_masks):
    units = lax.axis_size("ulysses")
    groups = lax.axis_size("dp")
    _, tok_rows, width = q_raw.shape
    seq_len = tok_rows * units
    slots = HEADS // units
    group_bits = groups.bit_length() - 1
    block_count = block_masks.shape[1]
    gain_scale = (groups * seq_len * HEADS) ** (-0.5)
    in_vmem = pl.BlockSpec(memory_space=pltpu.VMEM)
    in_hbm = pl.BlockSpec(memory_space=pltpu.HBM)
    anywhere = pl.BlockSpec(memory_space=pl.ANY)
    shard = jax.ShapeDtypeStruct((1, tok_rows, width), jnp.bfloat16)
    half = jnp.bfloat16
    full = jnp.float32
    small = jax.ShapeDtypeStruct((2, HEAD_DIM), full)
    dma = pltpu.SemaphoreType.DMA
    operands = (
        q_raw, k_raw, values, grad_out,
        q_gain.reshape(1, HEAD_DIM), k_gain.reshape(1, HEAD_DIM), block_masks.transpose(1, 2, 0),
    )
    landed, gain_grads = pl.pallas_call(
        functools.partial(exchange_kernel, units, groups, gain_scale),
        out_shape=(jax.ShapeDtypeStruct((HEADS, 3, tok_rows, HEAD_DIM), half), small),
        in_specs=[in_hbm] * 7,
        out_specs=(anywhere, in_vmem),
        scratch_shapes=[
            pltpu.VMEM((slots, units, 4, tok_rows, HEAD_DIM), half),
            pltpu.VMEM((slots, units, 4, tok_rows, HEAD_DIM), half),
            pltpu.VMEM((slots, units, 3, tok_rows, HEAD_DIM), half),
            pltpu.VMEM((units, 8, HEAD_DIM), full),
            pltpu.VMEM((max(1, group_bits), 2, 8, HEAD_DIM), full),
            pltpu.VMEM((8, HEAD_DIM), full),
            dma((slots,)),
            dma((slots, units)),
            dma((slots, units)),
            dma((slots, 4)),
            dma((slots, units)),
            dma((slots, units)),
            dma((slots,)),
            dma((units,)),
            dma((units,)),
            dma((max(1, group_bits),)),
            dma((max(1, group_bits),)),
            dma((3,)),
            pltpu.VMEM((1, HEAD_DIM), full),
            pltpu.VMEM((1, HEAD_DIM), full),
            pltpu.VMEM((block_count, block_count, HEADS), jnp.int32),
            pltpu.VMEM((block_count, seq_len), full),
            pltpu.VMEM((seq_len, HEAD_DIM), half),
            pltpu.VMEM((seq_len, HEAD_DIM), half),
            pltpu.VMEM((HEAD_DIM, seq_len), half),
            pltpu.VMEM((seq_len, HEAD_DIM), full),
            pltpu.VMEM((seq_len, HEAD_DIM), full),
            pltpu.VMEM((seq_len, HEAD_DIM), full),
            pltpu.VMEM((seq_len, QUERY_TILE), full),
            pltpu.VMEM((seq_len, QUERY_TILE), full),
            pltpu.VMEM((seq_len, QUERY_TILE), half),
            pltpu.VMEM((seq_len, QUERY_TILE), half),
        ],
        compiler_params=pltpu.CompilerParams(collective_id=0, has_side_effects=True, vmem_limit_bytes=KERNEL_BYTES),
    )(
        *(pltpu.with_memory_space_constraint(operand, pltpu.HBM) for operand in operands)
    )
    return pl.pallas_call(
        hand_on_kernel,
        out_shape=(shard, shard, shard, small),
        in_specs=[anywhere] * 2,
        out_specs=[in_hbm] * 4,
        scratch_shapes=[dma((3,)), dma(())],
        compiler_params=pltpu.CompilerParams(vmem_limit_bytes=2**20),
    )(landed, gain_grads)


def solution(mesh):
    units = mesh.shape["ulysses"]
    even = all(size == 2 ** (size.bit_length() - 1) for size in (units, mesh.shape["dp"]))

    def chosen(q_raw, *rest):
        if even and HEADS % units == 0 and q_raw.shape[:2] == (1, BLOCK):
            return exchange_body(q_raw, *rest)
        return body(q_raw, *rest)

    return jax.shard_map(
        chosen,
        mesh=mesh,
        in_specs=(
            P("dp", "ulysses", None),
            P("dp", "ulysses", None),
            P("dp", "ulysses", None),
            P("dp", "ulysses", None),
            P(),
            P(),
            P(),
        ),
        out_specs=(
            P("dp", "ulysses", None),
            P("dp", "ulysses", None),
            P("dp", "ulysses", None),
            P(),
        ),
        check_vma=False,
    )
```

```python
import functools
import math

import jax
import jax.numpy as jnp
from jax import lax
from jax.experimental import pallas as pl
from jax.experimental.pallas import tpu as pltpu
from jax.sharding import PartitionSpec as P

HEADS = 24
HEAD_DIM = 128
SPLITS = 8
BLOCK = 128
TILE = 512
ITEMS = 32


norm_eps = 1e-06
neg_fill = -1e30


def rms_norm(raw, gain):
    raw_float = raw.astype(jnp.float32)
    spread = jnp.sqrt(jnp.mean(raw_float * raw_float, axis=-1, keepdims=True) + norm_eps)
    return (raw_float, spread, (raw_float / spread * gain).astype(jnp.bfloat16))


def norm_back(raw_float, spread, gain, grad_normed):
    inner = jnp.sum(gain * grad_normed * raw_float, axis=-1, keepdims=True)
    return gain * grad_normed / spread - raw_float * inner / (HEAD_DIM * spread**3)


def dot_rows(left_side, right_side):
    return lax.dot_general(
        left_side, right_side, (((1,), (1,)), ((), ())), preferred_element_type=jnp.float32
    )


def dot_cols(left_side, right_side):
    return lax.dot_general(
        left_side, right_side, (((0,), (0,)), ((), ())), preferred_element_type=jnp.float32
    )


def rows_of(source, tile_index):
    return lax.dynamic_slice_in_dim(source, tile_index * TILE, TILE, 0)


def add_rows(target, addend, tile_index):
    return lax.dynamic_update_slice_in_dim(
        target, rows_of(target, tile_index) + addend, tile_index * TILE, 0
    )


def plan_items(block_masks, unit_count):
    block_count = block_masks.shape[1]
    per_unit = ITEMS // unit_count
    head_ids = jnp.arange(HEADS, dtype=jnp.int32)
    weight = jnp.sum(block_masks, axis=(1, 2))
    order = jnp.argsort(-(weight * HEADS + head_ids))
    heavy_heads = order[:SPLITS]
    light_heads = order[SPLITS:]
    counter = jnp.arange(2 * SPLITS, dtype=jnp.int32)
    item_head = jnp.concatenate([heavy_heads[counter // 2], light_heads])
    item_half = jnp.concatenate([1 + counter % 2, jnp.zeros((HEADS - SPLITS,), jnp.int32)])
    upper = jnp.sum(block_masks[:, : block_count // 2, :], axis=(1, 2))
    lower = weight - upper
    item_weight = jnp.where(
        item_half == 0,
        weight[item_head],
        jnp.where(item_half == 1, upper[item_head], lower[item_head]),
    )
    ranked = jnp.argsort(-(item_weight * ITEMS + jnp.arange(ITEMS, dtype=jnp.int32)))
    places = jnp.arange(ITEMS, dtype=jnp.int32)
    rounds = places // unit_count
    column = places % unit_count
    device = jnp.where(rounds % 2 == 0, column, unit_count - 1 - column)
    target = device * per_unit + rounds
    plan_head = jnp.zeros((ITEMS,), jnp.int32).at[target].set(item_head[ranked])
    plan_half = jnp.zeros((ITEMS,), jnp.int32).at[target].set(item_half[ranked])
    return (plan_head, plan_half)


def item_grads(columns, mask_head, half_code, q_gain, k_gain):
    seq_len = columns.shape[0]
    q_float, q_spread, q_normed = rms_norm(columns[:, :HEAD_DIM], q_gain)
    k_float, k_spread, k_normed = rms_norm(columns[:, HEAD_DIM : 2 * HEAD_DIM], k_gain)
    v_rows = columns[:, 2 * HEAD_DIM : 3 * HEAD_DIM]
    o_grads = columns[:, 3 * HEAD_DIM :]
    tile_count = seq_len // TILE
    tile_blocks = TILE // BLOCK
    active = (
        jnp.max(mask_head.reshape(tile_count, tile_blocks, tile_count, tile_blocks), axis=(1, 3))
        > 0
    )
    first_tile = jnp.where(half_code == 2, tile_count // 2, 0)
    last_tile = jnp.where(half_code == 1, tile_count // 2, tile_count)
    score_scale = HEAD_DIM ** (-0.5)

    def allowed_at(row_tile, col_tile):
        blocks = lax.dynamic_slice(
            mask_head, (row_tile * tile_blocks, col_tile * tile_blocks), (tile_blocks, tile_blocks)
        )
        return jnp.repeat(jnp.repeat(blocks, BLOCK, 0), BLOCK, 1) > 0

    def query_tile(row_tile, carry):
        grad_qn, grad_kn, grad_v = carry
        q_tile = rows_of(q_normed, row_tile)
        o_tile = rows_of(o_grads, row_tile)

        def stats_step(col_tile, stats):

            def stats_visit(stats_in):
                run_max, run_sum, run_dot = stats_in
                allowed = allowed_at(row_tile, col_tile)
                scores = jnp.where(
                    allowed, dot_rows(q_tile, rows_of(k_normed, col_tile)) * score_scale, neg_fill
                )
                grad_weights = dot_rows(o_tile, rows_of(v_rows, col_tile))
                new_max = jnp.maximum(run_max, jnp.max(scores, axis=1, keepdims=True))
                weights = jnp.where(allowed, jnp.exp(scores - new_max), 0.0)
                rescale = jnp.exp(run_max - new_max)
                return (
                    new_max,
                    run_sum * rescale + jnp.sum(weights, axis=1, keepdims=True),
                    run_dot * rescale + jnp.sum(weights * grad_weights, axis=1, keepdims=True),
                )

            return lax.cond(
                active[row_tile, col_tile], stats_visit, lambda unchanged: unchanged, stats
            )

        start = (
            jnp.full((TILE, 1), neg_fill, jnp.float32),
            jnp.zeros((TILE, 1), jnp.float32),
            jnp.zeros((TILE, 1), jnp.float32),
        )
        run_max, run_sum, run_dot = lax.fori_loop(0, tile_count, stats_step, start)
        log_total = run_max + jnp.log(run_sum)
        row_delta = run_dot / run_sum

        def grad_step(col_tile, inner):

            def grad_visit(inner_in):
                tile_dq, grad_keys, grad_vals = inner_in
                allowed = allowed_at(row_tile, col_tile)
                k_tile = rows_of(k_normed, col_tile)
                v_tile = rows_of(v_rows, col_tile)
                scores = jnp.where(allowed, dot_rows(q_tile, k_tile) * score_scale, neg_fill)
                weights = jnp.where(allowed, jnp.exp(scores - log_total), 0.0)
                grad_weights = dot_rows(o_tile, v_tile)
                grad_scores = weights * (grad_weights - row_delta)
                weights_half = weights.astype(jnp.bfloat16)
                scores_half = grad_scores.astype(jnp.bfloat16)
                tile_dq = (
                    tile_dq
                    + jnp.dot(scores_half, k_tile, preferred_element_type=jnp.float32) * score_scale
                )
                grad_keys = add_rows(
                    grad_keys, dot_cols(scores_half, q_tile) * score_scale, col_tile
                )
                grad_vals = add_rows(grad_vals, dot_cols(weights_half, o_tile), col_tile)
                return (tile_dq, grad_keys, grad_vals)

            return lax.cond(
                active[row_tile, col_tile], grad_visit, lambda unchanged: unchanged, inner
            )

        tile_dq, grad_kn, grad_v = lax.fori_loop(
            0, tile_count, grad_step, (jnp.zeros((TILE, HEAD_DIM), jnp.float32), grad_kn, grad_v)
        )
        grad_qn = lax.dynamic_update_slice_in_dim(grad_qn, tile_dq, row_tile * TILE, 0)
        return (grad_qn, grad_kn, grad_v)

    empty = jnp.zeros((seq_len, HEAD_DIM), jnp.float32)
    grad_qn, grad_kn, grad_v = lax.fori_loop(
        first_tile, last_tile, query_tile, (empty, empty, empty)
    )
    grad_q = norm_back(q_float, q_spread, q_gain, grad_qn)
    grad_k = norm_back(k_float, k_spread, k_gain, grad_kn)
    gain_part = jnp.stack(
        [
            jnp.sum(grad_qn * q_float / q_spread, axis=0),
            jnp.sum(grad_kn * k_float / k_spread, axis=0),
        ]
    )
    return (jnp.concatenate([grad_q, grad_k, grad_v], axis=1), gain_part)


def body(q_raw, k_raw, values, grad_out, q_gain, k_gain, block_masks):
    unit_count = lax.axis_size("ulysses")
    group_count = lax.axis_size("dp")
    device_rank = lax.axis_index("ulysses")
    videos_here, tok_rows, width = q_raw.shape
    seq_len = tok_rows * unit_count
    per_unit = ITEMS // unit_count
    item_heads, item_halves = plan_items(block_masks, unit_count)
    stacked = jnp.concatenate(
        [
            operand.reshape(videos_here, tok_rows, HEADS, HEAD_DIM)
            for operand in (q_raw, k_raw, values, grad_out)
        ],
        axis=3,
    )
    picked = jnp.take(stacked, item_heads, axis=2)
    outgoing = picked.transpose(2, 0, 1, 3).reshape(
        unit_count, per_unit, videos_here, tok_rows, 4 * HEAD_DIM
    )
    arrived = lax.all_to_all(outgoing, "ulysses", split_axis=0, concat_axis=3, tiled=True)
    results = []
    gain_total = jnp.zeros((2, HEAD_DIM), jnp.float32)
    for item_slot in range(per_unit):
        item_index = device_rank * per_unit + item_slot
        head_index = item_heads[item_index]
        half_code = item_halves[item_index]
        mask_head = lax.dynamic_index_in_dim(block_masks, head_index, 0, keepdims=False)
        item_grad, gain_part = item_grads(
            arrived[0, item_slot, 0], mask_head, half_code, q_gain, k_gain
        )
        video_rows = [item_grad]
        gain_total = gain_total + gain_part
        results.append(jnp.stack(video_rows))
    backward = jnp.stack(results)[None]
    returned = lax.all_to_all(
        backward.astype(jnp.bfloat16), "ulysses", split_axis=3, concat_axis=0, tiled=True
    ).astype(backward.dtype)
    returned = returned.reshape(ITEMS, videos_here, tok_rows, 3 * HEAD_DIM)
    selector = (item_heads[:, None] == jnp.arange(HEADS)[None, :]).astype(jnp.float32)
    merged = jnp.einsum("ih,ivtc->vthc", selector, returned, precision=lax.Precision.HIGHEST)
    grad_q_raw = merged[..., :HEAD_DIM].reshape(videos_here, tok_rows, width).astype(jnp.bfloat16)
    grad_k_raw = (
        merged[..., HEAD_DIM : 2 * HEAD_DIM]
        .reshape(videos_here, tok_rows, width)
        .astype(jnp.bfloat16)
    )
    grad_values = (
        merged[..., 2 * HEAD_DIM :].reshape(videos_here, tok_rows, width).astype(jnp.bfloat16)
    )
    summed = lax.psum(gain_total, ("dp", "ulysses"))
    gain_grads = summed * (group_count * videos_here * seq_len * HEADS) ** (-0.5)
    return (grad_q_raw, grad_k_raw, grad_values, gain_grads)


QUERY_TILE = 256
KERNEL_BYTES = 24 * 2**20
MESH = pl.DeviceIdType.MESH


def aligned(index, size):
    return pl.ds(pl.multiple_of(index * size, size), size)


def head_work(slot, arrived, results, gain_acc, gains, scratch):
    bias, q_norm, k_norm, k_cols, grad_qn, grad_kn, grad_v, scores, grads, probs_half, grads_half = scratch
    _, units, _, tok_rows, _ = arrived.shape
    seq_len = units * tok_rows
    block_count = seq_len // BLOCK
    tile_units = QUERY_TILE // tok_rows
    score_scale = HEAD_DIM ** (-0.5)
    exponent_scale = score_scale * math.log2(math.e)

    def rows_for(which):
        return arrived[slot, :, which].reshape(seq_len, HEAD_DIM)

    def put(which, grad):
        results[slot, :, which] = grad.astype(jnp.bfloat16).reshape(units, tok_rows, HEAD_DIM)

    def normed(which):
        raw = rows_for(which).astype(jnp.float32)
        inverse = 1.0 / jnp.sqrt(jnp.mean(raw * raw, axis=1, keepdims=True) + norm_eps)
        return raw * inverse * gains[which][...]

    q_norm[...] = normed(0).astype(jnp.bfloat16)
    k_float = normed(1)
    k_norm[...] = k_float.astype(jnp.bfloat16)
    k_cols[...] = k_float.T.astype(jnp.bfloat16)
    grad_kn[...] = jnp.zeros_like(grad_kn)
    grad_v[...] = jnp.zeros_like(grad_v)

    def tile_step(tile, carry):
        rows = aligned(tile, QUERY_TILE)
        q_tile = q_norm[rows, :]
        o_tile = arrived[slot, pl.ds(tile * tile_units, tile_units), 3].reshape(QUERY_TILE, HEAD_DIM)
        shifts = bias[:, rows]
        peak = jnp.full((1, QUERY_TILE), -jnp.inf, jnp.float32)
        for block in range(block_count):
            keys = pl.ds(block * BLOCK, BLOCK)
            block_scores = dot_rows(k_norm[keys, :], q_tile)
            scores[keys, :] = block_scores
            block_peak = jnp.max(block_scores, axis=0, keepdims=True) * exponent_scale
            peak = jnp.maximum(peak, block_peak + shifts[block : block + 1, :])
        total = jnp.zeros((1, QUERY_TILE), jnp.float32)
        row_dot = jnp.zeros((1, QUERY_TILE), jnp.float32)
        for block in range(block_count):
            keys = pl.ds(block * BLOCK, BLOCK)
            offset = shifts[block : block + 1, :] - peak
            weights = jnp.exp2(scores[keys, :] * exponent_scale + offset)
            grad_weights = dot_rows(arrived[slot, block, 2], o_tile)
            scores[keys, :] = weights
            grads[keys, :] = grad_weights
            total = total + jnp.sum(weights, axis=0, keepdims=True)
            row_dot = row_dot + jnp.sum(weights * grad_weights, axis=0, keepdims=True)
        inverse = 1.0 / total
        delta = row_dot * inverse
        for block in range(block_count):
            keys = pl.ds(block * BLOCK, BLOCK)
            weights = scores[keys, :] * inverse
            probs_half[keys, :] = weights.astype(jnp.bfloat16)
            grads_half[keys, :] = (weights * (grads[keys, :] - delta)).astype(jnp.bfloat16)
        grad_v[...] += jnp.dot(probs_half[...], o_tile, preferred_element_type=jnp.float32)
        grad_kn[...] += jnp.dot(grads_half[...], q_tile, preferred_element_type=jnp.float32)
        turned = jnp.dot(k_cols[...], grads_half[...], preferred_element_type=jnp.float32)
        grad_qn[rows, :] = turned.T
        return carry

    lax.fori_loop(0, seq_len // QUERY_TILE, tile_step, 0)
    put(2, grad_v[...])
    for which, grad_normed in ((0, grad_qn), (1, grad_kn)):
        raw = rows_for(which).astype(jnp.float32)
        inverse = 1.0 / jnp.sqrt(jnp.mean(raw * raw, axis=1, keepdims=True) + norm_eps)
        unit = raw * inverse
        grad = grad_normed[...] * score_scale
        gain_acc[which : which + 1, :] += jnp.sum(grad * unit, axis=0, keepdims=True)
        scaled = grad * gains[which][...]
        inner = jnp.mean(scaled * unit, axis=1, keepdims=True)
        put(which, (scaled - unit * inner) * inverse)


def exchange_kernel(
    units, groups, gain_scale,
    q_raw, k_raw, values, grad_out, q_gain_in, k_gain_in, masks_in,
    landed, out_gain,
    staged, arrived, results, gain_units, gain_groups, gain_acc,
    stage_sem, in_send, in_recv, in_own, out_send, out_recv, out_own,
    unit_send, unit_recv, group_send, group_recv, small_sem, q_gain, k_gain, masks, *scratch,
):
    me = lax.axis_index("ulysses")
    group = lax.axis_index("dp")
    slots = arrived.shape[0]
    sources = (q_raw, k_raw, values, grad_out)
    bits = units.bit_length() - 1
    group_bits = groups.bit_length() - 1

    def flipped(index, offset, count):
        places = (lax.rem(index // 2**bit + offset // 2**bit, 2) * 2**bit for bit in range(count))
        return sum(places, jnp.int32(0))

    def unit_at(offset):
        return flipped(me, offset, bits)

    offsets = sorted(range(1, units), key=lambda offset: (-(offset // 2).bit_count(), offset % 2, offset))

    def stage(slot, owner, which):
        return pltpu.make_async_copy(
            sources[which].at[0, :, aligned(owner * slots + slot, HEAD_DIM)],
            staged.at[slot, owner, which],
            stage_sem.at[slot],
        )

    def remote(source, target, send_sem, recv_sem, device):
        return pltpu.make_async_remote_copy(
            src_ref=source,
            dst_ref=target,
            send_sem=send_sem,
            recv_sem=recv_sem,
            device_id=device,
            device_id_type=MESH,
        )

    def inward(slot, offset):
        owner = unit_at(offset)
        return remote(
            staged.at[slot, owner], arrived.at[slot, me],
            in_send.at[slot, offset], in_recv.at[slot, offset], {"ulysses": owner},
        )

    def inward_own(slot, which):
        return pltpu.make_async_copy(
            sources[which].at[0, :, aligned(me * slots + slot, HEAD_DIM)],
            arrived.at[slot, me, which],
            in_own.at[slot, which],
        )

    def inward_from(slot, offset):
        owner = unit_at(offset)
        place = arrived.at[slot, owner]
        return remote(place, place, in_send.at[slot, offset], in_recv.at[slot, offset], {"ulysses": owner})

    def outward(slot, offset):
        owner = unit_at(offset)
        return remote(
            results.at[slot, owner], landed.at[me * slots + slot],
            out_send.at[slot, offset], out_recv.at[slot, offset], {"ulysses": owner},
        )

    def outward_own(slot):
        return pltpu.make_async_copy(
            results.at[slot, me], landed.at[me * slots + slot], out_own.at[slot]
        )

    def outward_from(slot, offset):
        owner = unit_at(offset)
        place = landed.at[owner * slots + slot]
        return remote(place, place, out_send.at[slot, offset], out_recv.at[slot, offset], {"ulysses": owner})

    def unit_gain(place, offset):
        block = gain_units.at[place]
        return remote(block, block, unit_send.at[offset], unit_recv.at[offset], {"ulysses": unit_at(offset)})

    def group_gain(bit):
        return remote(
            gain_groups.at[bit, 0], gain_groups.at[bit, 1],
            group_send.at[bit], group_recv.at[bit], {"dp": flipped(group, 2**bit, group_bits)},
        )

    small_copies = [
        pltpu.make_async_copy(source, target, small_sem.at[place])
        for place, (source, target) in enumerate(
            ((q_gain_in, q_gain), (k_gain_in, k_gain), (masks_in, masks))
        )
    ]
    barrier = pltpu.get_barrier_semaphore()
    for offset in offsets:
        pl.semaphore_signal(barrier, inc=1, device_id={"ulysses": unit_at(offset)}, device_id_type=MESH)
    for bit in range(group_bits):
        pl.semaphore_signal(
            barrier, inc=1, device_id={"dp": flipped(group, 2**bit, group_bits)}, device_id_type=MESH
        )

    def fetch_slot(slot, carry):
        for owner in range(units):
            for which in range(4):
                stage(slot, owner, which).start()
        return carry

    lax.fori_loop(0, slots, fetch_slot, 0)
    for copy in small_copies:
        copy.start()
    for slot in range(slots):
        for which in range(4):
            inward_own(slot, which).start()
    gain_acc[...] = jnp.zeros_like(gain_acc)
    pl.semaphore_wait(barrier, units - 1 + group_bits)

    def send_slot(slot, carry):
        pltpu.make_async_copy(staged.at[slot], staged.at[slot], stage_sem.at[slot]).wait()
        for offset in offsets:
            inward(slot, offset).start()
        return carry

    lax.fori_loop(0, slots, send_slot, 0)
    for copy in small_copies:
        copy.wait()
    bias = scratch[0]
    block_count = masks.shape[0]

    def work_slot(slot, carry):
        columns = lax.broadcasted_iota(jnp.int32, (block_count, HEADS), 1)
        for block in range(block_count):
            allowed = jnp.where(columns == me * slots + slot, masks[block].astype(jnp.float32), 0.0)
            allowed = jnp.sum(allowed, axis=1, keepdims=True)
            shift = jnp.where(allowed > 0.0, 0.0, -jnp.inf)
            bias[:, block * BLOCK : (block + 1) * BLOCK] = jnp.broadcast_to(shift, (block_count, BLOCK))
        for which in range(4):
            inward_own(slot, which).wait()
        for offset in offsets:
            inward_from(slot, offset).wait_recv()
        head_work(slot, arrived, results, gain_acc, (q_gain, k_gain), scratch)

        @pl.when(slot == slots - 1)
        def _():
            gain_sum = gain_acc[...]
            for bit in range(group_bits):
                gain_groups[bit, 0] = gain_sum
                group_gain(bit).start()
                group_gain(bit).wait_recv()
                gain_sum = gain_sum + gain_groups[bit, 1]
            gain_units[me] = gain_sum
            for offset in offsets:
                unit_gain(me, offset).start()

        for offset in offsets:
            outward(slot, offset).start()
        outward_own(slot).start()
        return carry

    lax.fori_loop(0, slots, work_slot, 0)

    for offset in offsets:
        unit_gain(unit_at(offset), offset).wait_recv()
    out_gain[...] = jnp.sum(gain_units[...], axis=0)[:2] * gain_scale

    def drain_slot(slot, carry):
        for offset in offsets:
            inward(slot, offset).wait_send()
            outward(slot, offset).wait_send()
            outward_from(slot, offset).wait_recv()
        outward_own(slot).wait()
        return carry

    lax.fori_loop(0, slots, drain_slot, 0)
    for offset in offsets:
        unit_gain(me, offset).wait_send()
    for bit in range(group_bits):
        group_gain(bit).wait_send()


def hand_on_kernel(landed, gain_in, out_q, out_k, out_v, out_gain, sems, gain_sem):
    targets = (out_q, out_k, out_v)
    gain_copy = pltpu.make_async_copy(gain_in, out_gain, gain_sem)
    gain_copy.start()
    for head in range(landed.shape[0]):
        for which in range(3):
            pltpu.make_async_copy(
                landed.at[head, which],
                targets[which].at[0, :, pl.ds(head * HEAD_DIM, HEAD_DIM)],
                sems.at[which],
            ).start()
    for which in range(3):
        pltpu.make_async_copy(targets[which], targets[which], sems.at[which]).wait()
    gain_copy.wait()


def exchange_body(q_raw, k_raw, values, grad_out, q_gain, k_gain, block_masks):
    units = lax.axis_size("ulysses")
    groups = lax.axis_size("dp")
    _, tok_rows, width = q_raw.shape
    seq_len = tok_rows * units
    slots = HEADS // units
    group_bits = groups.bit_length() - 1
    block_count = block_masks.shape[1]
    gain_scale = (groups * seq_len * HEADS) ** (-0.5)
    in_vmem = pl.BlockSpec(memory_space=pltpu.VMEM)
    in_hbm = pl.BlockSpec(memory_space=pltpu.HBM)
    anywhere = pl.BlockSpec(memory_space=pl.ANY)
    shard = jax.ShapeDtypeStruct((1, tok_rows, width), jnp.bfloat16)
    half = jnp.bfloat16
    full = jnp.float32
    small = jax.ShapeDtypeStruct((2, HEAD_DIM), full)
    dma = pltpu.SemaphoreType.DMA
    operands = (
        q_raw, k_raw, values, grad_out,
        q_gain.reshape(1, HEAD_DIM), k_gain.reshape(1, HEAD_DIM), block_masks.transpose(1, 2, 0),
    )
    landed, gain_grads = pl.pallas_call(
        functools.partial(exchange_kernel, units, groups, gain_scale),
        out_shape=(jax.ShapeDtypeStruct((HEADS, 3, tok_rows, HEAD_DIM), half), small),
        in_specs=[in_hbm] * 7,
        out_specs=(anywhere, in_vmem),
        scratch_shapes=[
            pltpu.VMEM((slots, units, 4, tok_rows, HEAD_DIM), half),
            pltpu.VMEM((slots, units, 4, tok_rows, HEAD_DIM), half),
            pltpu.VMEM((slots, units, 3, tok_rows, HEAD_DIM), half),
            pltpu.VMEM((units, 8, HEAD_DIM), full),
            pltpu.VMEM((max(1, group_bits), 2, 8, HEAD_DIM), full),
            pltpu.VMEM((8, HEAD_DIM), full),
            dma((slots,)),
            dma((slots, units)),
            dma((slots, units)),
            dma((slots, 4)),
            dma((slots, units)),
            dma((slots, units)),
            dma((slots,)),
            dma((units,)),
            dma((units,)),
            dma((max(1, group_bits),)),
            dma((max(1, group_bits),)),
            dma((3,)),
            pltpu.VMEM((1, HEAD_DIM), full),
            pltpu.VMEM((1, HEAD_DIM), full),
            pltpu.VMEM((block_count, block_count, HEADS), jnp.int32),
            pltpu.VMEM((block_count, seq_len), full),
            pltpu.VMEM((seq_len, HEAD_DIM), half),
            pltpu.VMEM((seq_len, HEAD_DIM), half),
            pltpu.VMEM((HEAD_DIM, seq_len), half),
            pltpu.VMEM((seq_len, HEAD_DIM), full),
            pltpu.VMEM((seq_len, HEAD_DIM), full),
            pltpu.VMEM((seq_len, HEAD_DIM), full),
            pltpu.VMEM((seq_len, QUERY_TILE), full),
            pltpu.VMEM((seq_len, QUERY_TILE), full),
            pltpu.VMEM((seq_len, QUERY_TILE), half),
            pltpu.VMEM((seq_len, QUERY_TILE), half),
        ],
        compiler_params=pltpu.CompilerParams(collective_id=0, has_side_effects=True, vmem_limit_bytes=KERNEL_BYTES),
    )(
        *(pltpu.with_memory_space_constraint(operand, pltpu.HBM) for operand in operands)
    )
    return pl.pallas_call(
        hand_on_kernel,
        out_shape=(shard, shard, shard, small),
        in_specs=[anywhere] * 2,
        out_specs=[in_hbm] * 4,
        scratch_shapes=[dma((3,)), dma(())],
        compiler_params=pltpu.CompilerParams(vmem_limit_bytes=2**20),
    )(landed, gain_grads)


def solution(mesh):
    units = mesh.shape["ulysses"]
    even = all(size == 2 ** (size.bit_length() - 1) for size in (units, mesh.shape["dp"]))

    def chosen(q_raw, *rest):
        if even and HEADS % units == 0 and q_raw.shape[:2] == (1, BLOCK):
            return exchange_body(q_raw, *rest)
        return body(q_raw, *rest)

    return jax.shard_map(
        chosen,
        mesh=mesh,
        in_specs=(
            P("dp", "ulysses", None),
            P("dp", "ulysses", None),
            P("dp", "ulysses", None),
            P("dp", "ulysses", None),
            P(),
            P(),
            P(),
        ),
        out_specs=(
            P("dp", "ulysses", None),
            P("dp", "ulysses", None),
            P("dp", "ulysses", None),
            P(),
        ),
        check_vma=False,
    )
```

```python
import functools
import math

import jax
import jax.numpy as jnp
from jax import lax
from jax.experimental import pallas as pl
from jax.experimental.pallas import tpu as pltpu
from jax.sharding import PartitionSpec as P

HEADS = 24
HEAD_DIM = 128
SPLITS = 8
BLOCK = 128
TILE = 512
ITEMS = 32


norm_eps = 1e-06
neg_fill = -1e30


def rms_norm(raw, gain):
    raw_float = raw.astype(jnp.float32)
    spread = jnp.sqrt(jnp.mean(raw_float * raw_float, axis=-1, keepdims=True) + norm_eps)
    return (raw_float, spread, (raw_float / spread * gain).astype(jnp.bfloat16))


def norm_back(raw_float, spread, gain, grad_normed):
    inner = jnp.sum(gain * grad_normed * raw_float, axis=-1, keepdims=True)
    return gain * grad_normed / spread - raw_float * inner / (HEAD_DIM * spread**3)


def dot_rows(left_side, right_side):
    return lax.dot_general(
        left_side, right_side, (((1,), (1,)), ((), ())), preferred_element_type=jnp.float32
    )


def dot_cols(left_side, right_side):
    return lax.dot_general(
        left_side, right_side, (((0,), (0,)), ((), ())), preferred_element_type=jnp.float32
    )


def rows_of(source, tile_index):
    return lax.dynamic_slice_in_dim(source, tile_index * TILE, TILE, 0)


def add_rows(target, addend, tile_index):
    return lax.dynamic_update_slice_in_dim(
        target, rows_of(target, tile_index) + addend, tile_index * TILE, 0
    )


def plan_items(block_masks, unit_count):
    block_count = block_masks.shape[1]
    per_unit = ITEMS // unit_count
    head_ids = jnp.arange(HEADS, dtype=jnp.int32)
    weight = jnp.sum(block_masks, axis=(1, 2))
    order = jnp.argsort(-(weight * HEADS + head_ids))
    heavy_heads = order[:SPLITS]
    light_heads = order[SPLITS:]
    counter = jnp.arange(2 * SPLITS, dtype=jnp.int32)
    item_head = jnp.concatenate([heavy_heads[counter // 2], light_heads])
    item_half = jnp.concatenate([1 + counter % 2, jnp.zeros((HEADS - SPLITS,), jnp.int32)])
    upper = jnp.sum(block_masks[:, : block_count // 2, :], axis=(1, 2))
    lower = weight - upper
    item_weight = jnp.where(
        item_half == 0,
        weight[item_head],
        jnp.where(item_half == 1, upper[item_head], lower[item_head]),
    )
    ranked = jnp.argsort(-(item_weight * ITEMS + jnp.arange(ITEMS, dtype=jnp.int32)))
    places = jnp.arange(ITEMS, dtype=jnp.int32)
    rounds = places // unit_count
    column = places % unit_count
    device = jnp.where(rounds % 2 == 0, column, unit_count - 1 - column)
    target = device * per_unit + rounds
    plan_head = jnp.zeros((ITEMS,), jnp.int32).at[target].set(item_head[ranked])
    plan_half = jnp.zeros((ITEMS,), jnp.int32).at[target].set(item_half[ranked])
    return (plan_head, plan_half)


def item_grads(columns, mask_head, half_code, q_gain, k_gain):
    seq_len = columns.shape[0]
    q_float, q_spread, q_normed = rms_norm(columns[:, :HEAD_DIM], q_gain)
    k_float, k_spread, k_normed = rms_norm(columns[:, HEAD_DIM : 2 * HEAD_DIM], k_gain)
    v_rows = columns[:, 2 * HEAD_DIM : 3 * HEAD_DIM]
    o_grads = columns[:, 3 * HEAD_DIM :]
    tile_count = seq_len // TILE
    tile_blocks = TILE // BLOCK
    active = (
        jnp.max(mask_head.reshape(tile_count, tile_blocks, tile_count, tile_blocks), axis=(1, 3))
        > 0
    )
    first_tile = jnp.where(half_code == 2, tile_count // 2, 0)
    last_tile = jnp.where(half_code == 1, tile_count // 2, tile_count)
    score_scale = HEAD_DIM ** (-0.5)

    def allowed_at(row_tile, col_tile):
        blocks = lax.dynamic_slice(
            mask_head, (row_tile * tile_blocks, col_tile * tile_blocks), (tile_blocks, tile_blocks)
        )
        return jnp.repeat(jnp.repeat(blocks, BLOCK, 0), BLOCK, 1) > 0

    def query_tile(row_tile, carry):
        grad_qn, grad_kn, grad_v = carry
        q_tile = rows_of(q_normed, row_tile)
        o_tile = rows_of(o_grads, row_tile)

        def stats_step(col_tile, stats):

            def stats_visit(stats_in):
                run_max, run_sum, run_dot = stats_in
                allowed = allowed_at(row_tile, col_tile)
                scores = jnp.where(
                    allowed, dot_rows(q_tile, rows_of(k_normed, col_tile)) * score_scale, neg_fill
                )
                grad_weights = dot_rows(o_tile, rows_of(v_rows, col_tile))
                new_max = jnp.maximum(run_max, jnp.max(scores, axis=1, keepdims=True))
                weights = jnp.where(allowed, jnp.exp(scores - new_max), 0.0)
                rescale = jnp.exp(run_max - new_max)
                return (
                    new_max,
                    run_sum * rescale + jnp.sum(weights, axis=1, keepdims=True),
                    run_dot * rescale + jnp.sum(weights * grad_weights, axis=1, keepdims=True),
                )

            return lax.cond(
                active[row_tile, col_tile], stats_visit, lambda unchanged: unchanged, stats
            )

        start = (
            jnp.full((TILE, 1), neg_fill, jnp.float32),
            jnp.zeros((TILE, 1), jnp.float32),
            jnp.zeros((TILE, 1), jnp.float32),
        )
        run_max, run_sum, run_dot = lax.fori_loop(0, tile_count, stats_step, start)
        log_total = run_max + jnp.log(run_sum)
        row_delta = run_dot / run_sum

        def grad_step(col_tile, inner):

            def grad_visit(inner_in):
                tile_dq, grad_keys, grad_vals = inner_in
                allowed = allowed_at(row_tile, col_tile)
                k_tile = rows_of(k_normed, col_tile)
                v_tile = rows_of(v_rows, col_tile)
                scores = jnp.where(allowed, dot_rows(q_tile, k_tile) * score_scale, neg_fill)
                weights = jnp.where(allowed, jnp.exp(scores - log_total), 0.0)
                grad_weights = dot_rows(o_tile, v_tile)
                grad_scores = weights * (grad_weights - row_delta)
                weights_half = weights.astype(jnp.bfloat16)
                scores_half = grad_scores.astype(jnp.bfloat16)
                tile_dq = (
                    tile_dq
                    + jnp.dot(scores_half, k_tile, preferred_element_type=jnp.float32) * score_scale
                )
                grad_keys = add_rows(
                    grad_keys, dot_cols(scores_half, q_tile) * score_scale, col_tile
                )
                grad_vals = add_rows(grad_vals, dot_cols(weights_half, o_tile), col_tile)
                return (tile_dq, grad_keys, grad_vals)

            return lax.cond(
                active[row_tile, col_tile], grad_visit, lambda unchanged: unchanged, inner
            )

        tile_dq, grad_kn, grad_v = lax.fori_loop(
            0, tile_count, grad_step, (jnp.zeros((TILE, HEAD_DIM), jnp.float32), grad_kn, grad_v)
        )
        grad_qn = lax.dynamic_update_slice_in_dim(grad_qn, tile_dq, row_tile * TILE, 0)
        return (grad_qn, grad_kn, grad_v)

    empty = jnp.zeros((seq_len, HEAD_DIM), jnp.float32)
    grad_qn, grad_kn, grad_v = lax.fori_loop(
        first_tile, last_tile, query_tile, (empty, empty, empty)
    )
    grad_q = norm_back(q_float, q_spread, q_gain, grad_qn)
    grad_k = norm_back(k_float, k_spread, k_gain, grad_kn)
    gain_part = jnp.stack(
        [
            jnp.sum(grad_qn * q_float / q_spread, axis=0),
            jnp.sum(grad_kn * k_float / k_spread, axis=0),
        ]
    )
    return (jnp.concatenate([grad_q, grad_k, grad_v], axis=1), gain_part)


def body(q_raw, k_raw, values, grad_out, q_gain, k_gain, block_masks):
    unit_count = lax.axis_size("ulysses")
    group_count = lax.axis_size("dp")
    device_rank = lax.axis_index("ulysses")
    videos_here, tok_rows, width = q_raw.shape
    seq_len = tok_rows * unit_count
    per_unit = ITEMS // unit_count
    item_heads, item_halves = plan_items(block_masks, unit_count)
    stacked = jnp.concatenate(
        [
            operand.reshape(videos_here, tok_rows, HEADS, HEAD_DIM)
            for operand in (q_raw, k_raw, values, grad_out)
        ],
        axis=3,
    )
    picked = jnp.take(stacked, item_heads, axis=2)
    outgoing = picked.transpose(2, 0, 1, 3).reshape(
        unit_count, per_unit, videos_here, tok_rows, 4 * HEAD_DIM
    )
    arrived = lax.all_to_all(outgoing, "ulysses", split_axis=0, concat_axis=3, tiled=True)
    results = []
    gain_total = jnp.zeros((2, HEAD_DIM), jnp.float32)
    for item_slot in range(per_unit):
        item_index = device_rank * per_unit + item_slot
        head_index = item_heads[item_index]
        half_code = item_halves[item_index]
        mask_head = lax.dynamic_index_in_dim(block_masks, head_index, 0, keepdims=False)
        item_grad, gain_part = item_grads(
            arrived[0, item_slot, 0], mask_head, half_code, q_gain, k_gain
        )
        video_rows = [item_grad]
        gain_total = gain_total + gain_part
        results.append(jnp.stack(video_rows))
    backward = jnp.stack(results)[None]
    returned = lax.all_to_all(
        backward.astype(jnp.bfloat16), "ulysses", split_axis=3, concat_axis=0, tiled=True
    ).astype(backward.dtype)
    returned = returned.reshape(ITEMS, videos_here, tok_rows, 3 * HEAD_DIM)
    selector = (item_heads[:, None] == jnp.arange(HEADS)[None, :]).astype(jnp.float32)
    merged = jnp.einsum("ih,ivtc->vthc", selector, returned, precision=lax.Precision.HIGHEST)
    grad_q_raw = merged[..., :HEAD_DIM].reshape(videos_here, tok_rows, width).astype(jnp.bfloat16)
    grad_k_raw = (
        merged[..., HEAD_DIM : 2 * HEAD_DIM]
        .reshape(videos_here, tok_rows, width)
        .astype(jnp.bfloat16)
    )
    grad_values = (
        merged[..., 2 * HEAD_DIM :].reshape(videos_here, tok_rows, width).astype(jnp.bfloat16)
    )
    summed = lax.psum(gain_total, ("dp", "ulysses"))
    gain_grads = summed * (group_count * videos_here * seq_len * HEADS) ** (-0.5)
    return (grad_q_raw, grad_k_raw, grad_values, gain_grads)


QUERY_TILE = 256
KERNEL_BYTES = 24 * 2**20
MESH = pl.DeviceIdType.MESH


def aligned(index, size):
    return pl.ds(pl.multiple_of(index * size, size), size)


def head_work(slot, arrived, results, gain_acc, gains, scratch):
    bias, q_norm, k_norm, k_cols, grad_qn, grad_kn, grad_v, scores, grads, probs_half, grads_half = scratch
    _, units, _, tok_rows, _ = arrived.shape
    seq_len = units * tok_rows
    block_count = seq_len // BLOCK
    tile_units = QUERY_TILE // tok_rows
    score_scale = HEAD_DIM ** (-0.5)
    exponent_scale = score_scale * math.log2(math.e)

    def rows_for(which):
        return arrived[slot, :, which].reshape(seq_len, HEAD_DIM)

    def put(which, grad):
        results[slot, :, which] = grad.astype(jnp.bfloat16).reshape(units, tok_rows, HEAD_DIM)

    def normed(which):
        raw = rows_for(which).astype(jnp.float32)
        inverse = 1.0 / jnp.sqrt(jnp.mean(raw * raw, axis=1, keepdims=True) + norm_eps)
        return raw * inverse * gains[which][...]

    q_norm[...] = normed(0).astype(jnp.bfloat16)
    k_float = normed(1)
    k_norm[...] = k_float.astype(jnp.bfloat16)
    k_cols[...] = k_float.T.astype(jnp.bfloat16)
    grad_kn[...] = jnp.zeros_like(grad_kn)
    grad_v[...] = jnp.zeros_like(grad_v)

    def tile_step(tile, carry):
        rows = aligned(tile, QUERY_TILE)
        q_tile = q_norm[rows, :]
        o_tile = arrived[slot, pl.ds(tile * tile_units, tile_units), 3].reshape(QUERY_TILE, HEAD_DIM)
        shifts = bias[:, rows]
        peak = jnp.full((1, QUERY_TILE), -jnp.inf, jnp.float32)
        for block in range(block_count):
            keys = pl.ds(block * BLOCK, BLOCK)
            block_scores = dot_rows(k_norm[keys, :], q_tile)
            scores[keys, :] = block_scores
            block_peak = jnp.max(block_scores, axis=0, keepdims=True) * exponent_scale
            peak = jnp.maximum(peak, block_peak + shifts[block : block + 1, :])
        total = jnp.zeros((1, QUERY_TILE), jnp.float32)
        row_dot = jnp.zeros((1, QUERY_TILE), jnp.float32)
        for block in range(block_count):
            keys = pl.ds(block * BLOCK, BLOCK)
            offset = shifts[block : block + 1, :] - peak
            weights = jnp.exp2(scores[keys, :] * exponent_scale + offset)
            grad_weights = dot_rows(arrived[slot, block, 2], o_tile)
            scores[keys, :] = weights
            grads[keys, :] = grad_weights
            total = total + jnp.sum(weights, axis=0, keepdims=True)
            row_dot = row_dot + jnp.sum(weights * grad_weights, axis=0, keepdims=True)
        inverse = 1.0 / total
        delta = row_dot * inverse
        for block in range(block_count):
            keys = pl.ds(block * BLOCK, BLOCK)
            weights = scores[keys, :] * inverse
            probs_half[keys, :] = weights.astype(jnp.bfloat16)
            grads_half[keys, :] = (weights * (grads[keys, :] - delta)).astype(jnp.bfloat16)
        grad_v[...] += jnp.dot(probs_half[...], o_tile, preferred_element_type=jnp.float32)
        grad_kn[...] += jnp.dot(grads_half[...], q_tile, preferred_element_type=jnp.float32)
        turned = jnp.dot(k_cols[...], grads_half[...], preferred_element_type=jnp.float32)
        grad_qn[rows, :] = turned.T
        return carry

    lax.fori_loop(0, seq_len // QUERY_TILE, tile_step, 0)
    put(2, grad_v[...])
    for which, grad_normed in ((0, grad_qn), (1, grad_kn)):
        raw = rows_for(which).astype(jnp.float32)
        inverse = 1.0 / jnp.sqrt(jnp.mean(raw * raw, axis=1, keepdims=True) + norm_eps)
        unit = raw * inverse
        grad = grad_normed[...] * score_scale
        gain_acc[which : which + 1, :] += jnp.sum(grad * unit, axis=0, keepdims=True)
        scaled = grad * gains[which][...]
        inner = jnp.mean(scaled * unit, axis=1, keepdims=True)
        put(which, (scaled - unit * inner) * inverse)


def exchange_kernel(
    units, groups, gain_scale,
    q_raw, k_raw, values, grad_out, q_gain_in, k_gain_in, masks_in,
    landed, out_gain,
    staged, arrived, results, gain_units, gain_groups, gain_acc,
    stage_sem, in_send, in_recv, in_own, out_send, out_recv, out_own,
    unit_send, unit_recv, group_send, group_recv, small_sem, q_gain, k_gain, masks, *scratch,
):
    me = lax.axis_index("ulysses")
    group = lax.axis_index("dp")
    slots = arrived.shape[0]
    sources = (q_raw, k_raw, values, grad_out)
    bits = units.bit_length() - 1
    group_bits = groups.bit_length() - 1

    def flipped(index, offset, count):
        places = (lax.rem(index // 2**bit + offset // 2**bit, 2) * 2**bit for bit in range(count))
        return sum(places, jnp.int32(0))

    def unit_at(offset):
        return flipped(me, offset, bits)

    offsets = sorted(range(1, units), key=lambda offset: (-(offset // 2).bit_count(), offset % 2, offset))

    def stage(slot, owner, which):
        return pltpu.make_async_copy(
            sources[which].at[0, :, aligned(owner * slots + slot, HEAD_DIM)],
            staged.at[slot, owner, which],
            stage_sem.at[slot, owner],
        )

    def remote(source, target, send_sem, recv_sem, device):
        return pltpu.make_async_remote_copy(
            src_ref=source,
            dst_ref=target,
            send_sem=send_sem,
            recv_sem=recv_sem,
            device_id=device,
            device_id_type=MESH,
        )

    def inward(slot, offset):
        owner = unit_at(offset)
        return remote(
            staged.at[slot, owner], arrived.at[slot, me],
            in_send.at[slot, offset], in_recv.at[slot, offset], {"ulysses": owner},
        )

    def inward_own(slot, which):
        return pltpu.make_async_copy(
            sources[which].at[0, :, aligned(me * slots + slot, HEAD_DIM)],
            arrived.at[slot, me, which],
            in_own.at[slot, which],
        )

    def inward_from(slot, offset):
        owner = unit_at(offset)
        place = arrived.at[slot, owner]
        return remote(place, place, in_send.at[slot, offset], in_recv.at[slot, offset], {"ulysses": owner})

    def outward(slot, offset):
        owner = unit_at(offset)
        return remote(
            results.at[slot, owner], landed.at[me * slots + slot],
            out_send.at[slot, offset], out_recv.at[slot, offset], {"ulysses": owner},
        )

    def outward_own(slot):
        return pltpu.make_async_copy(
            results.at[slot, me], landed.at[me * slots + slot], out_own.at[slot]
        )

    def outward_from(slot, offset):
        owner = unit_at(offset)
        place = landed.at[owner * slots + slot]
        return remote(place, place, out_send.at[slot, offset], out_recv.at[slot, offset], {"ulysses": owner})

    def unit_gain(place, offset):
        block = gain_units.at[place]
        return remote(block, block, unit_send.at[offset], unit_recv.at[offset], {"ulysses": unit_at(offset)})

    def group_gain(bit):
        return remote(
            gain_groups.at[bit, 0], gain_groups.at[bit, 1],
            group_send.at[bit], group_recv.at[bit], {"dp": flipped(group, 2**bit, group_bits)},
        )

    small_copies = [
        pltpu.make_async_copy(source, target, small_sem.at[place])
        for place, (source, target) in enumerate(
            ((q_gain_in, q_gain), (k_gain_in, k_gain), (masks_in, masks))
        )
    ]
    barrier = pltpu.get_barrier_semaphore()
    for offset in offsets:
        pl.semaphore_signal(barrier, inc=1, device_id={"ulysses": unit_at(offset)}, device_id_type=MESH)
    for bit in range(group_bits):
        pl.semaphore_signal(
            barrier, inc=1, device_id={"dp": flipped(group, 2**bit, group_bits)}, device_id_type=MESH
        )

    def fetch_slot(slot, carry):
        for offset in offsets:
            for which in range(4):
                stage(slot, unit_at(offset), which).start()
        return carry

    lax.fori_loop(0, slots, fetch_slot, 0)
    for copy in small_copies:
        copy.start()
    for slot in range(slots):
        for which in range(4):
            inward_own(slot, which).start()
    gain_acc[...] = jnp.zeros_like(gain_acc)
    pl.semaphore_wait(barrier, units - 1 + group_bits)

    def send_slot(slot, carry):
        for offset in offsets:
            block = staged.at[slot, unit_at(offset)]
            pltpu.make_async_copy(block, block, stage_sem.at[slot, unit_at(offset)]).wait()
            inward(slot, offset).start()
        return carry

    lax.fori_loop(0, slots, send_slot, 0)
    for copy in small_copies:
        copy.wait()
    bias = scratch[0]
    block_count = masks.shape[0]

    def work_slot(slot, carry):
        columns = lax.broadcasted_iota(jnp.int32, (block_count, HEADS), 1)
        for block in range(block_count):
            allowed = jnp.where(columns == me * slots + slot, masks[block].astype(jnp.float32), 0.0)
            allowed = jnp.sum(allowed, axis=1, keepdims=True)
            shift = jnp.where(allowed > 0.0, 0.0, -jnp.inf)
            bias[:, block * BLOCK : (block + 1) * BLOCK] = jnp.broadcast_to(shift, (block_count, BLOCK))
        for which in range(4):
            inward_own(slot, which).wait()
        for offset in offsets:
            inward_from(slot, offset).wait_recv()
        head_work(slot, arrived, results, gain_acc, (q_gain, k_gain), scratch)

        @pl.when(slot == slots - 1)
        def _():
            gain_sum = gain_acc[...]
            for bit in range(group_bits):
                gain_groups[bit, 0] = gain_sum
                group_gain(bit).start()
                group_gain(bit).wait_recv()
                gain_sum = gain_sum + gain_groups[bit, 1]
            gain_units[me] = gain_sum
            for offset in offsets:
                unit_gain(me, offset).start()

        for offset in offsets:
            outward(slot, offset).start()
        outward_own(slot).start()
        return carry

    lax.fori_loop(0, slots, work_slot, 0)

    for offset in offsets:
        unit_gain(unit_at(offset), offset).wait_recv()
    out_gain[...] = jnp.sum(gain_units[...], axis=0)[:2] * gain_scale

    def drain_slot(slot, carry):
        for offset in offsets:
            inward(slot, offset).wait_send()
            outward(slot, offset).wait_send()
            outward_from(slot, offset).wait_recv()
        outward_own(slot).wait()
        return carry

    lax.fori_loop(0, slots, drain_slot, 0)
    for offset in offsets:
        unit_gain(me, offset).wait_send()
    for bit in range(group_bits):
        group_gain(bit).wait_send()


def hand_on_kernel(landed, gain_in, out_q, out_k, out_v, out_gain, sems, gain_sem):
    targets = (out_q, out_k, out_v)
    gain_copy = pltpu.make_async_copy(gain_in, out_gain, gain_sem)
    gain_copy.start()
    for head in range(landed.shape[0]):
        for which in range(3):
            pltpu.make_async_copy(
                landed.at[head, which],
                targets[which].at[0, :, pl.ds(head * HEAD_DIM, HEAD_DIM)],
                sems.at[which],
            ).start()
    for which in range(3):
        pltpu.make_async_copy(targets[which], targets[which], sems.at[which]).wait()
    gain_copy.wait()


def exchange_body(q_raw, k_raw, values, grad_out, q_gain, k_gain, block_masks):
    units = lax.axis_size("ulysses")
    groups = lax.axis_size("dp")
    _, tok_rows, width = q_raw.shape
    seq_len = tok_rows * units
    slots = HEADS // units
    group_bits = groups.bit_length() - 1
    block_count = block_masks.shape[1]
    gain_scale = (groups * seq_len * HEADS) ** (-0.5)
    in_vmem = pl.BlockSpec(memory_space=pltpu.VMEM)
    in_hbm = pl.BlockSpec(memory_space=pltpu.HBM)
    anywhere = pl.BlockSpec(memory_space=pl.ANY)
    shard = jax.ShapeDtypeStruct((1, tok_rows, width), jnp.bfloat16)
    half = jnp.bfloat16
    full = jnp.float32
    small = jax.ShapeDtypeStruct((2, HEAD_DIM), full)
    dma = pltpu.SemaphoreType.DMA
    operands = (
        q_raw, k_raw, values, grad_out,
        q_gain.reshape(1, HEAD_DIM), k_gain.reshape(1, HEAD_DIM), block_masks.transpose(1, 2, 0),
    )
    landed, gain_grads = pl.pallas_call(
        functools.partial(exchange_kernel, units, groups, gain_scale),
        out_shape=(jax.ShapeDtypeStruct((HEADS, 3, tok_rows, HEAD_DIM), half), small),
        in_specs=[in_hbm] * 7,
        out_specs=(anywhere, in_vmem),
        scratch_shapes=[
            pltpu.VMEM((slots, units, 4, tok_rows, HEAD_DIM), half),
            pltpu.VMEM((slots, units, 4, tok_rows, HEAD_DIM), half),
            pltpu.VMEM((slots, units, 3, tok_rows, HEAD_DIM), half),
            pltpu.VMEM((units, 8, HEAD_DIM), full),
            pltpu.VMEM((max(1, group_bits), 2, 8, HEAD_DIM), full),
            pltpu.VMEM((8, HEAD_DIM), full),
            dma((slots, units)),
            dma((slots, units)),
            dma((slots, units)),
            dma((slots, 4)),
            dma((slots, units)),
            dma((slots, units)),
            dma((slots,)),
            dma((units,)),
            dma((units,)),
            dma((max(1, group_bits),)),
            dma((max(1, group_bits),)),
            dma((3,)),
            pltpu.VMEM((1, HEAD_DIM), full),
            pltpu.VMEM((1, HEAD_DIM), full),
            pltpu.VMEM((block_count, block_count, HEADS), jnp.int32),
            pltpu.VMEM((block_count, seq_len), full),
            pltpu.VMEM((seq_len, HEAD_DIM), half),
            pltpu.VMEM((seq_len, HEAD_DIM), half),
            pltpu.VMEM((HEAD_DIM, seq_len), half),
            pltpu.VMEM((seq_len, HEAD_DIM), full),
            pltpu.VMEM((seq_len, HEAD_DIM), full),
            pltpu.VMEM((seq_len, HEAD_DIM), full),
            pltpu.VMEM((seq_len, QUERY_TILE), full),
            pltpu.VMEM((seq_len, QUERY_TILE), full),
            pltpu.VMEM((seq_len, QUERY_TILE), half),
            pltpu.VMEM((seq_len, QUERY_TILE), half),
        ],
        compiler_params=pltpu.CompilerParams(collective_id=0, has_side_effects=True, vmem_limit_bytes=KERNEL_BYTES),
    )(
        *(pltpu.with_memory_space_constraint(operand, pltpu.HBM) for operand in operands)
    )
    return pl.pallas_call(
        hand_on_kernel,
        out_shape=(shard, shard, shard, small),
        in_specs=[anywhere] * 2,
        out_specs=[in_hbm] * 4,
        scratch_shapes=[dma((3,)), dma(())],
        compiler_params=pltpu.CompilerParams(vmem_limit_bytes=2**20),
    )(landed, gain_grads)


def solution(mesh):
    units = mesh.shape["ulysses"]
    even = all(size == 2 ** (size.bit_length() - 1) for size in (units, mesh.shape["dp"]))

    def chosen(q_raw, *rest):
        if even and HEADS % units == 0 and q_raw.shape[:2] == (1, BLOCK):
            return exchange_body(q_raw, *rest)
        return body(q_raw, *rest)

    return jax.shard_map(
        chosen,
        mesh=mesh,
        in_specs=(
            P("dp", "ulysses", None),
            P("dp", "ulysses", None),
            P("dp", "ulysses", None),
            P("dp", "ulysses", None),
            P(),
            P(),
            P(),
        ),
        out_specs=(
            P("dp", "ulysses", None),
            P("dp", "ulysses", None),
            P("dp", "ulysses", None),
            P(),
        ),
        check_vma=False,
    )
```
